32 devices in a mesh: ctx: 8 (over y, x, core), kvh: 4 (over z).
Axes of the slice: x: 2, y: 2, z: 4, core: 2. Of those that a mesh axis runs over, the one named last changes fastest.
Arguments:
- query_heads: bfloat16 [16384, 4096], P('ctx', 'kvh'), may hold values from -8 to 8
- key_heads: bfloat16 [16384, 1024], P('ctx', 'kvh'), may hold values from -4.5 to 4.5
- value_head_rows: bfloat16 [16384, 1024], P('ctx', 'kvh'), may hold values from -6 to 6
- out_weight: bfloat16 [4096, 4096], P('kvh'), may hold values from -0.09375 to 0.09375
- piece_lengths: int32 [16], replicated, may hold values from 1 to 4096, 16384 in all
- block_order: int32 [128], replicated, may hold values from 0 to 127, as said below
Outputs:
- mixed: bfloat16 [16384, 4096], P(('ctx', 'kvh'))
The draws below stay inside these ranges and needn't reach their ends.
Inputs may be any that keep to these rules, and one draw needn't show every extreme that they name: `block_order`: a permutation of the blocks; slot d * 16 + s * 2 + j with 0 <= j < 2 holds a block of the contiguous range s * 16 to (s + 1) * 16 - 1. `piece_lengths`: they sum to 16384.
All inputs are finite; a program needn't handle non-finite values.
Results may differ from the reference program's by a relative error of at most 0.013.
Values may be sent and summed in bfloat16 or wider, within the bound.
A program may use at most 128 MiB of HBM per device.

```python
import math
import jax
import jax.numpy as jnp
import numpy as np
from jax import lax

D = 4096
QUERY_HEAD_COUNT = 32
KEY_VALUE_HEADS = 8
HEAD_SIZE = 128
BLK = 128
MOST = 4096
PACKED_TOKENS = 16384
NPIECE = 16
NBLK = 128
BPD = 16
PER = 2
N_CTX = 8
N_KVH = 4


def draw_key_heads(key, part):
    final_output = jnp.clip(jax.random.normal(jax.random.fold_in(key, 22), (PACKED_TOKENS, KEY_VALUE_HEADS * HEAD_SIZE), jnp.float32), -4.5, 4.5)
    return final_output.astype(jnp.bfloat16)


def draw_query_heads(key, part):
    final_output = jnp.clip(jax.random.normal(jax.random.fold_in(key, 24), (PACKED_TOKENS, QUERY_HEAD_COUNT * HEAD_SIZE), jnp.float32), -4.5, 4.5)
    return final_output.astype(jnp.bfloat16)


def shard_permutation(subkey):
    return jax.random.permutation(subkey, BPD)


def draw_block_order(key, part):
    subkeys = jax.random.split(jax.random.fold_in(key, 31), N_CTX)
    perms = jax.vmap(shard_permutation)(subkeys).astype(jnp.int32)
    shifted = perms.reshape(N_CTX, N_CTX, PER) + (jnp.arange(N_CTX, dtype=jnp.int32) * BPD)[:, None, None]
    return jnp.transpose(shifted, (1, 0, 2)).reshape(NBLK).astype(jnp.int32)


def block_levels(stream_key, shape, pieces, smallest, largest):
    loudness, own = 1.0, jax.random.fold_in(stream_key, 6)
    for position, blocks in pieces:
        steps = jnp.exp(jax.random.uniform(jax.random.fold_in(own, position), (blocks,), jnp.float32, smallest / len(pieces), largest / len(pieces)))
        loudness = loudness * jnp.repeat(steps, shape[position] // blocks).reshape([-1 if axis == position else 1 for axis in range(len(shape))])
    return loudness


def profile(number_of, total, reach, skew):
    loads = [(1 << 20) // math.isqrt(rank ** skew) + 1 for rank in range(2, number_of + 1)]
    spare, counts = total - reach - (number_of - 1), [1] * (number_of - 1)
    while spare > 0:
        free = [i for i in range(number_of - 1) if counts[i] < reach]
        whole, left = sum([loads[i] for i in free]), spare
        for i in free:
            more = min(reach - counts[i], max(1, left * loads[i] // whole), spare)
            counts[i] = counts[i] + more
            spare = spare - more
    return np.array([reach] + counts)


def uneven(key, number_of, total, limit, lean):
    if number_of == 2:
        one = jax.random.randint(key, (), max(1, total - limit), min(limit, total - 1) + 1)
        return jnp.stack([one, total - one])
    tallies = jnp.asarray(profile(number_of, total, limit, lean), jnp.int32)
    twos = (number_of - 1) // 2
    source_of, receiver = tallies[1:1 + 2 * twos:2], tallies[2:2 + 2 * twos:2]
    slack = jnp.minimum(source_of - 1, limit - receiver)
    moved = jax.random.randint(jax.random.fold_in(key, 1), (twos,), 0, 1 << 20) % (slack + 1)
    tallies = tallies.at[1:1 + 2 * twos:2].set(source_of - moved).at[2:2 + 2 * twos:2].set(receiver + moved)
    return tallies[jax.random.permutation(jax.random.fold_in(key, 2), number_of)]


def scatter_about(rng, shape, scale, most, cuts=(), kind=jnp.bfloat16):
    drawn = scale * jax.random.normal(rng, shape, jnp.float32)
    if cuts:
        drawn = drawn * block_levels(rng, shape, cuts, -0.22, 0.18)
    return jnp.clip(drawn, -most, most).astype(kind)


def setup_inputs(seed: int = 0) -> dict:
    streams_of = jax.random.split(jax.random.key(seed), 7)
    query_heads = draw_query_heads(jax.random.fold_in(streams_of[6], 71), 0)
    key_heads = draw_key_heads(jax.random.fold_in(streams_of[6], 71), 0)
    value_head_rows = scatter_about(streams_of[2], (PACKED_TOKENS, KEY_VALUE_HEADS * HEAD_SIZE), 1.0, 6.0, ((0, 8), (1, 4)))
    out_weight = scatter_about(streams_of[3], (QUERY_HEAD_COUNT * HEAD_SIZE, D), (QUERY_HEAD_COUNT * HEAD_SIZE) ** -0.5, 0.09375, ((0, 4),))
    piece_lengths = uneven(streams_of[4], NPIECE, PACKED_TOKENS, MOST, 2).astype(jnp.int32)
    block_order = draw_block_order(jax.random.fold_in(streams_of[6], 71), 0)
    return dict(query_heads=query_heads, key_heads=key_heads, value_head_rows=value_head_rows, out_weight=out_weight, piece_lengths=piece_lengths, block_order=block_order)


def piece_starts(positions, piece_lengths):
    piece_ends = jnp.cumsum(piece_lengths).astype(jnp.int32)
    chosen = jnp.where(piece_ends[None, :] <= positions[:, None], piece_lengths[None, :], 0)
    return jnp.sum(chosen, axis=1).astype(jnp.int32)


def attend(query_block, key_window, value_window, query_pos, key_pos, query_start):
    groups = key_window.shape[1] // HEAD_SIZE
    per_group = query_block.shape[1] // key_window.shape[1]
    query_four = query_block.reshape(query_block.shape[0], groups, per_group, HEAD_SIZE).astype(jnp.float32)
    key_three = key_window.reshape(-1, groups, HEAD_SIZE).astype(jnp.float32)
    value_three = value_window.reshape(-1, groups, HEAD_SIZE).astype(jnp.float32)
    scores = jnp.einsum("qgjd,kgd->gjqk", query_four, key_three) * (1.0 / (HEAD_SIZE ** 0.5))
    allowed = (key_pos[None, :] >= query_start[:, None]) & (key_pos[None, :] <= query_pos[:, None])
    masked = jnp.where(allowed, scores, -jnp.inf)
    highest = jnp.max(masked, axis=-1, keepdims=True)
    weights = jnp.exp(masked - highest)
    totals = jnp.sum(weights, axis=-1)
    rounded = weights.astype(jnp.bfloat16).astype(jnp.float32)
    summed = jnp.einsum("gjqk,kgd->qgjd", rounded, value_three)
    scaled = summed / jnp.transpose(totals, (2, 0, 1))[..., None]
    return scaled.reshape(query_block.shape[0], -1).astype(jnp.bfloat16)


def reference(query_heads, key_heads, value_head_rows, out_weight, piece_lengths, block_order):
    positions = jnp.arange(PACKED_TOKENS, dtype=jnp.int32)
    start_all = piece_starts(positions, piece_lengths)
    zero_rows = jnp.zeros((MOST, key_heads.shape[1]), jnp.bfloat16)
    key_padded = jnp.concatenate([zero_rows, key_heads], axis=0)
    value_padded = jnp.concatenate([zero_rows, value_head_rows], axis=0)
    offsets = jnp.arange(BLK, dtype=jnp.int32)
    window_offsets = jnp.arange(MOST + BLK, dtype=jnp.int32)

    def attend_one(block_id):
        first_row = (block_id * BLK).astype(jnp.int32)
        query_block = lax.dynamic_slice_in_dim(query_heads, first_row, BLK, 0)
        key_window = lax.dynamic_slice_in_dim(key_padded, first_row, MOST + BLK, 0)
        value_window = lax.dynamic_slice_in_dim(value_padded, first_row, MOST + BLK, 0)
        query_pos = first_row + offsets
        key_pos = first_row - MOST + window_offsets
        query_start = lax.dynamic_slice_in_dim(start_all, first_row, BLK, 0)
        return attend(query_block, key_window, value_window, query_pos, key_pos, query_start)

    attended = lax.map(attend_one, jnp.arange(NBLK, dtype=jnp.int32))
    arranged = jnp.take(attended, block_order, axis=0).reshape(PACKED_TOKENS, QUERY_HEAD_COUNT * HEAD_SIZE)
    width = QUERY_HEAD_COUNT * HEAD_SIZE // N_KVH
    final_output = jnp.zeros((PACKED_TOKENS, D), jnp.float32)
    for group_index in range(N_KVH):
        partial_sum = jnp.dot(arranged[:, group_index * width:(group_index + 1) * width],
                              out_weight[group_index * width:(group_index + 1) * width, :],
                              preferred_element_type=jnp.float32).astype(jnp.bfloat16)
        partial_sum = lax.optimization_barrier(partial_sum)
        final_output = final_output + partial_sum.astype(jnp.float32)
    return final_output.astype(jnp.bfloat16)
```

```python
import functools
import math
import jax
import jax.numpy as jnp
from jax import lax
from jax.experimental import pallas as pl
from jax.experimental.pallas import tpu as pltpu
from jax.sharding import Mesh, PartitionSpec as P

HEAD_SIZE = 128
BLK = 128
CHUNK = 512
CTX = ("cg", "cp")
SCALE = math.log2(math.e) / HEAD_SIZE**0.5
NEG = -1e30


def attend_kernel(ids, lows, ends, lengths, q_ref, kv_ref, out_ref, q_four, top, acc):
    step = pl.program_id(0)
    heads = q_ref.shape[1] // HEAD_SIZE
    tokens = kv_ref.shape[0]
    first_row = ids[step] * BLK
    low = lows[step]
    for h in range(heads):
        q_four[h * BLK : (h + 1) * BLK, :] = q_ref[:, h * HEAD_SIZE : (h + 1) * HEAD_SIZE]
    top[...] = jnp.full_like(top, NEG)
    acc[...] = jnp.zeros_like(acc)
    query_pos = first_row + lax.broadcasted_iota(jnp.int32, (BLK, 1), 0)
    start = jnp.zeros((BLK, 1), jnp.int32)
    for p in range(ends.shape[0]):
        start = start + jnp.where(ends[p] <= query_pos, lengths[p], 0)
    count = (first_row + BLK - low + CHUNK - 1) // CHUNK

    def one(j, carry):
        begin = low + j * CHUNK
        at = pl.multiple_of(jnp.minimum(begin, tokens - CHUNK), BLK)
        key_pos = at + lax.broadcasted_iota(jnp.int32, (BLK, CHUNK), 1)
        allowed = (key_pos >= jnp.maximum(start, begin)) & (key_pos <= query_pos)
        bias = jnp.where(allowed, 0.0, NEG)
        keys = kv_ref[pl.ds(at, CHUNK), :HEAD_SIZE]
        values = kv_ref[pl.ds(at, CHUNK), HEAD_SIZE:]
        wide = jnp.concatenate([values, jnp.ones_like(values)], axis=1)
        for h in range(heads):
            rows = slice(h * BLK, (h + 1) * BLK)
            s = lax.dot_general(
                q_four[rows, :], keys, (((1,), (1,)), ((), ())), preferred_element_type=jnp.float32
            )
            s = s * SCALE + bias
            old = top[rows, :]
            new = jnp.maximum(old, jnp.max(s, axis=1, keepdims=True))
            top[rows, :] = new
            weights = jnp.exp2(s - new[:, :1]).astype(jnp.bfloat16)
            keep = jnp.exp2(old - new)
            keep = jnp.concatenate([keep, keep], axis=1)
            acc[rows, :] = acc[rows, :] * keep + jnp.dot(
                weights, wide, preferred_element_type=jnp.float32
            )
        return carry

    lax.fori_loop(0, count, one, 0)
    for h in range(heads):
        rows = slice(h * BLK, (h + 1) * BLK)
        out_ref[:, h * HEAD_SIZE : (h + 1) * HEAD_SIZE] = (
            acc[rows, :HEAD_SIZE] / acc[rows, HEAD_SIZE:]
        ).astype(jnp.bfloat16)


def attend(ids, lows, ends, lengths, query, kv):
    rows, width = query.shape
    tokens = kv.shape[0]
    stacked = BLK * width // HEAD_SIZE
    return pl.pallas_call(
        attend_kernel,
        out_shape=jax.ShapeDtypeStruct((rows, width), jnp.bfloat16),
        grid_spec=pltpu.PrefetchScalarGridSpec(
            num_scalar_prefetch=4,
            grid=(rows // BLK,),
            in_specs=[
                pl.BlockSpec((BLK, width), lambda i, *_: (i, 0)),
                pl.BlockSpec(memory_space=pltpu.VMEM),
            ],
            out_specs=pl.BlockSpec((BLK, width), lambda i, *_: (i, 0)),
            scratch_shapes=[
                pltpu.VMEM((stacked, HEAD_SIZE), jnp.bfloat16),
                pltpu.VMEM((stacked, HEAD_SIZE), jnp.float32),
                pltpu.VMEM((stacked, 2 * HEAD_SIZE), jnp.float32),
            ],
        ),
        compiler_params=pltpu.CompilerParams(vmem_limit_bytes=40 * 1024 * 1024),
        cost_estimate=pl.CostEstimate(
            flops=4 * rows * width * 1500, bytes_accessed=tokens * 512, transcendentals=rows * 4 * 1500
        ),
    )(ids, lows, ends, lengths, query, kv)


def body(query_heads, key_heads, value_head_rows, out_weight, piece_lengths, block_order):
    num_ctx = lax.axis_size(CTX)
    num_cg = lax.axis_size("cg")
    num_kvh = lax.axis_size("kvh")
    ctx_index = lax.axis_index(CTX)
    core = lax.axis_index("cp")
    tokens_dev = query_heads.shape[0]
    block_count = tokens_dev // BLK
    per_pair = block_count // num_ctx
    groups = key_heads.shape[1] // HEAD_SIZE
    width = query_heads.shape[1] // groups

    ends = jnp.cumsum(piece_lengths).astype(jnp.int32)
    owned = lax.dynamic_slice_in_dim(block_order, ctx_index * block_count, block_count, 0)
    first_rows = owned * BLK
    lows = jnp.sum(jnp.where(ends[None, :] <= first_rows[:, None], piece_lengths[None, :], 0), axis=1)
    lows = (lows // BLK * BLK).astype(jnp.int32)

    gathered_kv = []
    for g in range(groups):
        cols = slice(g * HEAD_SIZE, (g + 1) * HEAD_SIZE)
        pair = jnp.concatenate([key_heads[:, cols], value_head_rows[:, cols]], axis=1)
        if gathered_kv:
            pair, gathered_kv[-1] = lax.optimization_barrier((pair, gathered_kv[-1]))
        gathered_kv.append(lax.all_gather(pair, CTX, axis=0, tiled=True))

    pair_table = block_order.reshape(num_ctx, num_ctx, per_pair)
    sent_ids = lax.dynamic_index_in_dim(pair_table, ctx_index, 1, keepdims=False)
    local_ids = sent_ids - ctx_index * block_count
    outgoing = jnp.take(query_heads.reshape(block_count, BLK, -1), local_ids, axis=0)
    arrived = lax.all_to_all(outgoing, CTX, split_axis=0, concat_axis=0, tiled=True)
    arrived = arrived.reshape(tokens_dev, -1)

    half = out_weight.shape[1] // 2
    part = width // num_cg
    mine_w = lax.dynamic_slice_in_dim(out_weight, core * half, half, 1)
    weights = []
    last = gathered_kv[-1]
    for g in range(groups):
        piece = lax.dynamic_slice_in_dim(mine_w, g * width + lax.axis_index("cg") * part, part, 0)
        piece, last = lax.optimization_barrier((piece, last))
        weights.append(lax.all_gather(piece, ("kvh", "cg"), axis=0, tiled=True))
    gathered_kv[-1] = last

    swap = [(0, 1), (1, 0)]
    own, other = [], []
    for g in range(groups):
        attended = attend(
            owned, lows, ends, piece_lengths, arrived[:, g * width : (g + 1) * width], gathered_kv[g]
        )
        rows = lax.all_to_all(attended, "kvh", split_axis=0, concat_axis=1, tiled=True)
        own.append(rows)
        other.append(lax.ppermute(rows, "cp", swap))

    def project(parts):
        total = 0.0
        for x, w in zip(parts, weights):
            total = total + jnp.dot(x, w, preferred_element_type=jnp.float32)
        return total.astype(jnp.bfloat16)

    back = lax.ppermute(project(other), "cp", swap)
    here = project(own)
    return jnp.where(
        core == 0,
        jnp.concatenate([here, back], axis=1),
        jnp.concatenate([back, here], axis=1),
    )


def solution(mesh):
    num_ctx, num_kvh = mesh.devices.shape
    split = Mesh(mesh.devices.reshape(num_ctx // 2, 2, num_kvh), ("cg", "cp", "kvh"))
    placed = (P(CTX, "kvh"), P(CTX, "kvh"), P(CTX, "kvh"), P("kvh", None), P(), P())
    return jax.shard_map(
        body, mesh=split, in_specs=placed, out_specs=P(("cg", "cp", "kvh"), None), check_vma=False
    )
```
